32 devices in a mesh: rep: 2 (over x), seq: 16 (over z, y, core).
Axes of the slice: x: 2, y: 2, z: 4, core: 2. Of those that a mesh axis runs over, the one named last changes fastest.
Arguments:
- q_stream: bfloat16 [4096, 8192], P(('rep', 'seq')), parts along dimension 0, may hold values from -6 to 6
- k_stream: bfloat16 [4096, 8192], P(('rep', 'seq')), parts along dimension 0, may hold values from -6 to 6
- v_stream: bfloat16 [4096, 8192], P(('rep', 'seq')), parts along dimension 0, may hold values from -6 to 6
- feat_filter: float32 [3, 3, 8192], replicated, may hold values from -3.5 to 3.5
- long_filter: bfloat16 [512, 128], replicated, may hold values from -0.5 to 0.5
- skip_gain: float32 [8192], replicated, may hold values from -3 to 3
Outputs:
- mixed: bfloat16 [4096, 8192], P(('rep', 'seq')), parts along dimension 0
The draws below stay inside these ranges and needn't reach their ends.
There are 2 independent parts, one for each index of `rep`. The reference program is written for one: setup_inputs(seed, part) draws one part's arguments, and reference() takes and returns one part's arrays. A program takes and returns all parts, laid end to end along the dimension named above; an argument that names none is the same for every part. Nothing has to cross between parts.
All inputs are finite; a program needn't handle non-finite values.
Results may differ from the reference program's by a relative error of at most 0.005.
Values may be sent and summed in bfloat16 or wider, within the bound.
A program may use at most 128 MiB of HBM per device.

```python
import math
import jax
import jax.numpy as jnp
from jax import lax

D = 8192
GROUP_CH = 16
FILT = 128
FEAT = 3
GROUPS = 512
SEQ_LEN = 2048


def shard_levels(own_key, extent, cuts, least, high):
    loudness = 1.0
    for position, blocks in cuts:
        heights = jax.random.uniform(jax.random.fold_in(jax.random.fold_in(own_key, 6), position), (blocks,), jnp.float32, least / len(cuts), high / len(cuts))
        loudness = loudness * jnp.repeat(jnp.exp(heights), extent[position] // blocks).reshape((-1,) + (1,) * (len(extent) - 1 - position))
    return loudness


def noise(stream_key, shape, scale, limit, cuts=(), kind=jnp.bfloat16):
    level = shard_levels(stream_key, shape, cuts, -0.22, 0.18) if cuts else 1.0
    drawn = jax.random.normal(stream_key, shape, jnp.float32) * scale * level
    return jnp.minimum(jnp.maximum(drawn, -limit), limit).astype(kind)


def setup_inputs(seed: int = 0, part: int = 0) -> dict:
    key_list = jax.random.split(jax.random.key(seed), 7)
    part_keys = jax.random.split(jax.random.fold_in(key_list[6], part), 7)
    return {
        "q_stream": noise(part_keys[0], (SEQ_LEN, D), 1.0, 6.0, ((0, 16),)),
        "k_stream": noise(part_keys[1], (SEQ_LEN, D), 1.0, 6.0, ((0, 16),)),
        "v_stream": noise(part_keys[2], (SEQ_LEN, D), 1.0, 6.0, ((0, 16),)),
        "feat_filter": noise(key_list[3], (3, FEAT, D), FEAT ** -0.5, 3.5, (), jnp.float32),
        "long_filter": noise(key_list[4], (GROUPS, FILT), FILT ** -0.5, 0.5),
        "skip_gain": noise(key_list[5], (D,), 0.5, 3.0, (), jnp.float32),
    }


def featurize(stream, taps):
    length = stream.shape[0]
    padded = jnp.pad(stream.astype(jnp.float32), ((FEAT - 1, 0), (0, 0)))
    total = taps[0] * padded[FEAT - 1:FEAT - 1 + length]
    for j in range(1, FEAT):
        total = total + taps[j] * padded[FEAT - 1 - j:FEAT - 1 - j + length]
    return total


def reference(q_stream, k_stream, v_stream, feat_filter, long_filter, skip_gain):
    length = q_stream.shape[0]
    block = math.gcd(D, 512)
    count = D // block
    expanded = jnp.repeat(long_filter.astype(jnp.float32), GROUP_CH, axis=0).T

    def split(stream):
        return stream.reshape(length, count, block).transpose(1, 0, 2)

    taps_feat = feat_filter.reshape(3, FEAT, count, block).transpose(2, 0, 1, 3)
    taps_long = expanded.reshape(FILT, count, block).transpose(1, 0, 2)
    skips = skip_gain.reshape(count, block)

    def one_block(items):
        query, keys, values, tfeat, tlong, skip = items
        q_feat = featurize(query, tfeat[0])
        k_feat = featurize(keys, tfeat[1])
        v_feat = featurize(values, tfeat[2])
        gated = (k_feat * v_feat).astype(jnp.bfloat16)
        gated_f = gated.astype(jnp.float32)
        padded = jnp.pad(gated_f, ((FILT - 1, 0), (0, 0)))

        def add_tap(j, total):
            return total + tlong[j] * lax.dynamic_slice_in_dim(padded, FILT - 1 - j, length, 0)

        conv = lax.fori_loop(0, FILT, add_tap, jnp.zeros((length, block), jnp.float32))
        return (q_feat * (conv + skip * gated_f)).astype(jnp.bfloat16)

    result = lax.map(one_block, (split(q_stream), split(k_stream), split(v_stream), taps_feat, taps_long, skips))
    return result.transpose(1, 0, 2).reshape(length, D)
```

```python
import functools

import jax
import jax.numpy as jnp
from jax import lax
from jax.experimental import pallas as pl
from jax.experimental.pallas import tpu as pltpu
from jax.sharding import PartitionSpec as P

GROUP_CH = 16
FILT = 128
FEAT = 3
LANES = 128
SUB = 16
CHUNK = 512
EARLY = 2
MESH = pl.DeviceIdType.MESH


def shifted(rim, x):
    ext = jnp.concatenate([rim, x], axis=0)
    return pltpu.roll(ext, 1, 0)[8:], pltpu.roll(ext, 2, 0)[8:]


def featurize(x, rim, taps):
    x = x.astype(jnp.float32)
    one, two = shifted(rim, x)
    return taps[0] * x + taps[1] * one + taps[2] * two


def kernel(
    n, q_hbm, k_hbm, v_hbm, feat_hbm, long_hbm, skip_hbm, out_hbm,
    q, k, v, feat, filt, skip, ends, rim_out, rim_in, gated, prev, mixed, toep,
    in_sem, end_sem, par_sem, send_sem, recv_sem, out_sem,
):
    chunks, rows, width = gated.shape
    tiles = width // LANES
    groups = filt.shape[0]
    me = lax.axis_index("seq")
    right, left = lax.rem(me + 1, n), lax.rem(me + n - 1, n)
    has_left, has_right = me > 0, me < n - 1

    barrier = pltpu.get_barrier_semaphore()

    @pl.when(has_left)
    def _():
        pl.semaphore_signal(barrier, inc=1, device_id={"seq": left}, device_id_type=MESH)

    streams = ((k_hbm, k), (v_hbm, v), (q_hbm, q))

    def end_copy(i):
        return pltpu.make_async_copy(
            streams[i][0].at[pl.ds(rows - 8, 8)], ends.at[i], end_sem.at[i])

    def in_copy(i, c):
        cols = pl.ds(pl.multiple_of(c * width, width), width)
        return pltpu.make_async_copy(
            streams[i][0].at[:, cols], streams[i][1].at[c], in_sem.at[i, c])

    params = ((feat_hbm, feat), (long_hbm, filt), (skip_hbm, skip))

    def par_copy(i):
        return pltpu.make_async_copy(params[i][0], params[i][1], par_sem.at[i])

    for i in range(3):
        end_copy(i).start()
    for c in range(EARLY):
        in_copy(0, c).start()
        in_copy(1, c).start()
        if c == 0:
            par_copy(0).start()

    @pl.loop(EARLY, chunks)
    def _(c):
        in_copy(0, c).start()
        in_copy(1, c).start()

    par_copy(1).start()
    par_copy(2).start()

    @pl.loop(0, chunks)
    def _(c):
        in_copy(2, c).start()

    def remote(src, dst, slot):
        return pltpu.make_async_remote_copy(
            src_ref=src, dst_ref=dst, send_sem=send_sem.at[slot],
            recv_sem=recv_sem.at[slot], device_id={"seq": right}, device_id_type=MESH)

    def rim_copy():
        return remote(rim_out, rim_in, chunks + EARLY)

    def whole_copy(c):
        return remote(gated.at[c], prev.at[c], c)

    def body_copy(c):
        part = pl.ds(16, rows - 16)
        return remote(gated.at[c, part], prev.at[c, part], c)

    def head_copy(c):
        part = pl.ds(0, 16)
        return remote(gated.at[c, part], prev.at[c, part], chunks + c)

    for i in range(3):
        end_copy(i).wait()
    row = lax.broadcasted_iota(jnp.int32, (8, LANES), 0)

    @pl.loop(0, chunks)
    def _(c):
        for t in range(tiles):
            cols = pl.ds(pl.multiple_of(c * width + t * LANES, LANES), LANES)
            last = [ends[i, :, cols].astype(jnp.float32) for i in range(3)]
            packed = jnp.where(
                row < 2, pltpu.roll(last[0], 2, 0),
                jnp.where(row < 4, pltpu.roll(last[1], 4, 0), pltpu.roll(last[2], 6, 0)))
            rim_out[:, cols] = packed.astype(jnp.bfloat16)

    @pl.when(has_right)
    def _():
        pl.semaphore_wait(barrier, 1)
        rim_copy().start()

    def taps_of(i, cols):
        return [feat[i, pl.ds(j, 1), cols] for j in range(FEAT)]

    def rim_of(i, cols):
        x = rim_in[:, cols].astype(jnp.float32)
        return pltpu.roll(x, 6 - 2 * i, 0)

    def columns(c, t):
        return pl.ds(pl.multiple_of(c * width + t * LANES, LANES), LANES)

    def gate(c, t, first, count, k_rim, v_rim):
        cols = columns(c, t)
        part, lanes = pl.ds(first, count), pl.ds(t * LANES, LANES)
        k_feat = featurize(k[c, part, lanes], k_rim, taps_of(1, cols))
        v_feat = featurize(v[c, part, lanes], v_rim, taps_of(2, cols))
        return (k_feat * v_feat).astype(jnp.bfloat16)

    zeros = jnp.zeros((8, LANES), jnp.float32)
    par_copy(0).wait()
    for c in range(EARLY):
        in_copy(0, c).wait()
        in_copy(1, c).wait()
        for t in range(tiles):
            lanes = pl.ds(t * LANES, LANES)
            gated[c, pl.ds(16, rows - 16), lanes] = gate(c, t, 0, rows, zeros, zeros)[16:]

        @pl.when(has_right)
        def _():
            body_copy(c).start()

    @pl.when(has_left)
    def _():
        rim_copy().wait_recv()

    @pl.when(jnp.logical_not(has_left))
    def _():
        rim_in[...] = jnp.zeros_like(rim_in)

        @pl.loop(0, chunks)
        def _(c):
            prev[c] = jnp.zeros((rows, width), jnp.bfloat16)

    for c in range(EARLY):
        for t in range(tiles):
            cols = columns(c, t)
            gated[c, pl.ds(0, 16), pl.ds(t * LANES, LANES)] = gate(
                c, t, 0, 16, rim_of(0, cols), rim_of(1, cols))

        @pl.when(has_right)
        def _():
            head_copy(c).start()

    @pl.loop(EARLY, chunks)
    def _(c):
        in_copy(0, c).wait()
        in_copy(1, c).wait()
        for t in range(tiles):
            cols = columns(c, t)
            gated[c, :, pl.ds(t * LANES, LANES)] = gate(
                c, t, 0, rows, rim_of(0, cols), rim_of(1, cols))

        @pl.when(has_right)
        def _():
            whole_copy(c).start()

    par_copy(1).wait()
    par_copy(2).wait()
    taps = lax.broadcasted_iota(jnp.int32, (FILT, 2 * LANES), 0)
    place = lax.broadcasted_iota(jnp.int32, (FILT, 2 * LANES), 1)
    total = taps + place
    for b in range(SUB):
        onehot = jnp.where(total == FILT + b, 1.0, 0.0).astype(jnp.bfloat16)
        moved = jnp.dot(filt[...], onehot, preferred_element_type=jnp.float32)
        for r in range(2):
            toep[r, pl.ds(b, groups, stride=SUB), :] = moved[:, r * LANES:(r + 1) * LANES]

    lane_group = lax.broadcasted_iota(jnp.int32, (SUB, LANES), 1) // GROUP_CH
    per_tile = LANES // GROUP_CH
    blocks = rows // SUB
    depth = FILT + SUB

    def mix(c):
        for t in range(tiles):
            cols, lanes = columns(c, t), pl.ds(t * LANES, LANES)
            first = pl.multiple_of((c * tiles + t) * LANES, LANES)
            own = gated[c, :, lanes]
            window = jnp.concatenate([prev[c, :, lanes], own], axis=0)
            left_part = toep[0, pl.ds(first, LANES), :].astype(jnp.bfloat16)
            right_part = toep[1, pl.ds(first, LANES), :].astype(jnp.bfloat16)
            lhs = jnp.concatenate([left_part, right_part[:, :depth - LANES]], axis=1)
            rhs = jnp.concatenate(
                [window[a * SUB:a * SUB + depth] for a in range(blocks)], axis=1)
            every = jnp.dot(lhs, rhs, preferred_element_type=jnp.float32)
            conv = []
            for a in range(blocks):
                mine = every[:SUB, a * LANES:(a + 1) * LANES]
                for g in range(1, per_tile):
                    mine = jnp.where(
                        lane_group == g,
                        every[g * SUB:(g + 1) * SUB, a * LANES:(a + 1) * LANES], mine)
                conv.append(mine)
            conv = jnp.concatenate(conv, axis=0)
            q_feat = featurize(q[c, :, lanes], rim_of(2, cols), taps_of(0, cols))
            direct = skip[:, cols] * own.astype(jnp.float32)
            mixed[c, :, lanes] = (q_feat * (conv + direct)).astype(jnp.bfloat16)

    def out_copy(c):
        cols = pl.ds(pl.multiple_of(c * width, width), width)
        return pltpu.make_async_copy(mixed.at[c], out_hbm.at[:, cols], out_sem.at[c])

    for c in range(EARLY):
        @pl.when(has_left)
        def _():
            body_copy(c).wait_recv()
            head_copy(c).wait_recv()

        in_copy(2, c).wait()
        mix(c)
        out_copy(c).start()

    @pl.loop(EARLY, chunks)
    def _(c):
        @pl.when(has_left)
        def _():
            whole_copy(c).wait_recv()

        in_copy(2, c).wait()
        mix(c)
        out_copy(c).start()

    @pl.when(has_right)
    def _():
        rim_copy().wait_send()
        for c in range(EARLY):
            body_copy(c).wait_send()
            head_copy(c).wait_send()

        @pl.loop(EARLY, chunks)
        def _(c):
            whole_copy(c).wait_send()

    @pl.loop(0, chunks)
    def _(c):
        out_copy(c).wait()


def shards(n, q_stream, k_stream, v_stream, feat_filter, long_filter, skip_gain):
    rows, channels = q_stream.shape
    groups = long_filter.shape[0]
    chunks = channels // CHUNK
    cut = pltpu.VMEM((chunks, rows, CHUNK), jnp.bfloat16)
    dma = pltpu.SemaphoreType.DMA
    return pl.pallas_call(
        functools.partial(kernel, n),
        out_shape=jax.ShapeDtypeStruct((rows, channels), jnp.bfloat16),
        in_specs=[pl.BlockSpec(memory_space=pl.ANY)] * 6,
        out_specs=pl.BlockSpec(memory_space=pl.ANY),
        scratch_shapes=[
            cut, cut, cut,
            pltpu.VMEM(feat_filter.shape, jnp.float32),
            pltpu.VMEM(long_filter.shape, jnp.bfloat16),
            pltpu.VMEM((1, channels), jnp.float32),
            pltpu.VMEM((3, 8, channels), jnp.bfloat16),
            pltpu.VMEM((8, channels), jnp.bfloat16),
            pltpu.VMEM((8, channels), jnp.bfloat16),
            cut, cut, cut,
            pltpu.VMEM((2, groups * SUB, LANES), jnp.float32),
            dma((3, chunks)), dma((3,)), dma((3,)),
            dma((chunks + EARLY + 1,)), dma((chunks + EARLY + 1,)), dma((chunks,)),
        ],
        compiler_params=pltpu.CompilerParams(collective_id=0, has_side_effects=True),
    )(q_stream, k_stream, v_stream, feat_filter, long_filter, skip_gain.reshape(1, channels))


def solution(mesh):
    n = mesh.shape["seq"]
    rows = P(("rep", "seq"), None)
    return jax.shard_map(
        functools.partial(shards, n), mesh=mesh,
        in_specs=(rows, rows, rows, P(), P(), P()), out_specs=rows, check_vma=False)
```

```python
import functools

import jax
import jax.numpy as jnp
from jax import lax
from jax.experimental import pallas as pl
from jax.experimental.pallas import tpu as pltpu
from jax.sharding import PartitionSpec as P

GROUP_CH = 16
FILT = 128
FEAT = 3
LANES = 128
SUB = 16
CHUNK = 256
EARLY = 4
GRANT = 58 << 20
MESH = pl.DeviceIdType.MESH


def shifted(rim, x):
    ext = jnp.concatenate([rim, x], axis=0)
    return pltpu.roll(ext, 1, 0)[8:], pltpu.roll(ext, 2, 0)[8:]


def featurize(x, rim, taps):
    x = x.astype(jnp.float32)
    one, two = shifted(rim, x)
    return taps[0] * x + taps[1] * one + taps[2] * two


def kernel(
    n, q_hbm, k_hbm, v_hbm, feat_hbm, long_hbm, skip_hbm, mixed,
    q, k, v, feat, filt, skip, ends, rim_out, rim_in, gated, prev, toep,
    in_sem, end_sem, par_sem, send_sem, recv_sem,
):
    chunks, rows, width = gated.shape
    tiles = width // LANES
    groups = filt.shape[0]
    me = lax.axis_index("seq")
    right, left = lax.rem(me + 1, n), lax.rem(me + n - 1, n)
    has_left, has_right = me > 0, me < n - 1

    barrier = pltpu.get_barrier_semaphore()

    @pl.when(has_left)
    def _():
        pl.semaphore_signal(barrier, inc=1, device_id={"seq": left}, device_id_type=MESH)

    streams = ((k_hbm, k), (v_hbm, v), (q_hbm, q))

    def end_copy(i):
        return pltpu.make_async_copy(
            streams[i][0].at[pl.ds(rows - 8, 8)], ends.at[i], end_sem.at[i])

    def in_copy(i, c):
        cols = pl.ds(pl.multiple_of(c * width, width), width)
        return pltpu.make_async_copy(
            streams[i][0].at[:, cols], streams[i][1].at[c], in_sem.at[i, c])

    params = ((feat_hbm, feat), (long_hbm, filt), (skip_hbm, skip))

    def par_copy(i):
        return pltpu.make_async_copy(params[i][0], params[i][1], par_sem.at[i])

    for i in range(3):
        end_copy(i).start()
    for c in range(EARLY):
        in_copy(0, c).start()
        in_copy(1, c).start()
        if c == 0:
            par_copy(0).start()

    @pl.loop(EARLY, chunks)
    def _(c):
        in_copy(0, c).start()
        in_copy(1, c).start()

    par_copy(1).start()
    par_copy(2).start()

    @pl.loop(0, chunks)
    def _(c):
        in_copy(2, c).start()

    def remote(src, dst, slot):
        return pltpu.make_async_remote_copy(
            src_ref=src, dst_ref=dst, send_sem=send_sem.at[slot],
            recv_sem=recv_sem.at[slot], device_id={"seq": right}, device_id_type=MESH)

    def rim_copy():
        return remote(rim_out, rim_in, chunks + EARLY)

    def whole_copy(c):
        return remote(gated.at[c], prev.at[c], c)

    def body_copy(c):
        part = pl.ds(16, rows - 16)
        return remote(gated.at[c, part], prev.at[c, part], c)

    def head_copy(c):
        part = pl.ds(0, 16)
        return remote(gated.at[c, part], prev.at[c, part], chunks + c)

    for i in range(3):
        end_copy(i).wait()
    row = lax.broadcasted_iota(jnp.int32, (8, LANES), 0)

    @pl.loop(0, chunks)
    def _(c):
        for t in range(tiles):
            cols = pl.ds(pl.multiple_of(c * width + t * LANES, LANES), LANES)
            last = [ends[i, :, cols].astype(jnp.float32) for i in range(3)]
            packed = jnp.where(
                row < 2, pltpu.roll(last[0], 2, 0),
                jnp.where(row < 4, pltpu.roll(last[1], 4, 0), pltpu.roll(last[2], 6, 0)))
            rim_out[:, cols] = packed.astype(jnp.bfloat16)

    @pl.when(has_right)
    def _():
        pl.semaphore_wait(barrier, 1)
        rim_copy().start()

    def taps_of(i, cols):
        return [feat[i, pl.ds(j, 1), cols] for j in range(FEAT)]

    def rim_of(i, cols):
        x = rim_in[:, cols].astype(jnp.float32)
        return pltpu.roll(x, 6 - 2 * i, 0)

    def columns(c, t):
        return pl.ds(pl.multiple_of(c * width + t * LANES, LANES), LANES)

    def gate(c, t, first, count, k_rim, v_rim):
        cols = columns(c, t)
        part, lanes = pl.ds(first, count), pl.ds(t * LANES, LANES)
        k_feat = featurize(k[c, part, lanes], k_rim, taps_of(1, cols))
        v_feat = featurize(v[c, part, lanes], v_rim, taps_of(2, cols))
        return (k_feat * v_feat).astype(jnp.bfloat16)

    zeros = jnp.zeros((8, LANES), jnp.float32)
    par_copy(0).wait()
    for c in range(EARLY):
        in_copy(0, c).wait()
        in_copy(1, c).wait()
        for t in range(tiles):
            lanes = pl.ds(t * LANES, LANES)
            gated[c, pl.ds(16, rows - 16), lanes] = gate(c, t, 0, rows, zeros, zeros)[16:]

        @pl.when(has_right)
        def _():
            body_copy(c).start()

    @pl.when(has_left)
    def _():
        rim_copy().wait_recv()

    @pl.when(jnp.logical_not(has_left))
    def _():
        rim_in[...] = jnp.zeros_like(rim_in)

        @pl.loop(0, chunks)
        def _(c):
            prev[c] = jnp.zeros((rows, width), jnp.bfloat16)

    for c in range(EARLY):
        for t in range(tiles):
            cols = columns(c, t)
            gated[c, pl.ds(0, 16), pl.ds(t * LANES, LANES)] = gate(
                c, t, 0, 16, rim_of(0, cols), rim_of(1, cols))

        @pl.when(has_right)
        def _():
            head_copy(c).start()

    @pl.loop(EARLY, chunks)
    def _(c):
        in_copy(0, c).wait()
        in_copy(1, c).wait()
        for t in range(tiles):
            cols = columns(c, t)
            gated[c, :, pl.ds(t * LANES, LANES)] = gate(
                c, t, 0, rows, rim_of(0, cols), rim_of(1, cols))

        @pl.when(has_right)
        def _():
            whole_copy(c).start()

    par_copy(1).wait()
    par_copy(2).wait()
    taps = lax.broadcasted_iota(jnp.int32, (FILT, 2 * LANES), 0)
    place = lax.broadcasted_iota(jnp.int32, (FILT, 2 * LANES), 1)
    total = taps + place
    for b in range(SUB):
        onehot = jnp.where(total == FILT + b, 1.0, 0.0).astype(jnp.bfloat16)
        moved = jnp.dot(filt[...], onehot, preferred_element_type=jnp.float32)
        for r in range(2):
            toep[r, pl.ds(b, groups, stride=SUB), :] = moved[:, r * LANES:(r + 1) * LANES]

    lane_group = lax.broadcasted_iota(jnp.int32, (SUB, LANES), 1) // GROUP_CH
    per_tile = LANES // GROUP_CH
    blocks = rows // SUB
    depth = FILT + SUB

    def mix(c):
        for t in range(tiles):
            cols, lanes = columns(c, t), pl.ds(t * LANES, LANES)
            first = pl.multiple_of((c * tiles + t) * LANES, LANES)
            own = gated[c, :, lanes]
            window = jnp.concatenate([prev[c, :, lanes], own], axis=0)
            left_part = toep[0, pl.ds(first, LANES), :].astype(jnp.bfloat16)
            right_part = toep[1, pl.ds(first, LANES), :].astype(jnp.bfloat16)
            lhs = jnp.concatenate([left_part, right_part[:, :depth - LANES]], axis=1)
            rhs = jnp.concatenate(
                [window[a * SUB:a * SUB + depth] for a in range(blocks)], axis=1)
            every = jnp.dot(lhs, rhs, preferred_element_type=jnp.float32)
            conv = []
            for a in range(blocks):
                mine = every[:SUB, a * LANES:(a + 1) * LANES]
                for g in range(1, per_tile):
                    mine = jnp.where(
                        lane_group == g,
                        every[g * SUB:(g + 1) * SUB, a * LANES:(a + 1) * LANES], mine)
                conv.append(mine)
            conv = jnp.concatenate(conv, axis=0)
            q_feat = featurize(q[c, :, lanes], rim_of(2, cols), taps_of(0, cols))
            direct = skip[:, cols] * own.astype(jnp.float32)
            mixed[c, :, lanes] = (q_feat * (conv + direct)).astype(jnp.bfloat16)

    for c in range(EARLY):
        @pl.when(has_left)
        def _():
            body_copy(c).wait_recv()
            head_copy(c).wait_recv()

        in_copy(2, c).wait()
        mix(c)

    @pl.loop(EARLY, chunks)
    def _(c):
        @pl.when(has_left)
        def _():
            whole_copy(c).wait_recv()

        in_copy(2, c).wait()
        mix(c)

    @pl.when(has_right)
    def _():
        rim_copy().wait_send()
        for c in range(EARLY):
            body_copy(c).wait_send()
            head_copy(c).wait_send()

        @pl.loop(EARLY, chunks)
        def _(c):
            whole_copy(c).wait_send()


def drain(mixed, out_hbm, sem):
    chunks, _, width = mixed.shape

    def copy(c):
        return pltpu.make_async_copy(
            mixed.at[c], out_hbm.at[:, c * width:(c + 1) * width], sem.at[c])

    for c in range(chunks):
        copy(c).start()
    for c in range(chunks):
        copy(c).wait()


def shards(n, q_stream, k_stream, v_stream, feat_filter, long_filter, skip_gain):
    rows, channels = q_stream.shape
    groups = long_filter.shape[0]
    chunks = channels // CHUNK
    cut = pltpu.VMEM((chunks, rows, CHUNK), jnp.bfloat16)
    dma = pltpu.SemaphoreType.DMA
    mixed = pl.pallas_call(
        functools.partial(kernel, n),
        out_shape=cut,
        in_specs=[pl.BlockSpec(memory_space=pltpu.HBM)] * 6,
        out_specs=pl.BlockSpec(memory_space=pltpu.VMEM),
        scratch_shapes=[
            cut, cut, cut,
            pltpu.VMEM(feat_filter.shape, jnp.float32),
            pltpu.VMEM(long_filter.shape, jnp.bfloat16),
            pltpu.VMEM((1, channels), jnp.float32),
            pltpu.VMEM((3, 8, channels), jnp.bfloat16),
            pltpu.VMEM((8, channels), jnp.bfloat16),
            pltpu.VMEM((8, channels), jnp.bfloat16),
            cut, cut,
            pltpu.VMEM((2, groups * SUB, LANES), jnp.float32),
            dma((3, chunks)), dma((3,)), dma((3,)),
            dma((chunks + EARLY + 1,)), dma((chunks + EARLY + 1,)),
        ],
        compiler_params=pltpu.CompilerParams(
            collective_id=0, has_side_effects=True, vmem_limit_bytes=GRANT),
    )(q_stream, k_stream, v_stream, feat_filter, long_filter, skip_gain.reshape(1, channels))
    return pl.pallas_call(
        drain,
        out_shape=jax.ShapeDtypeStruct((rows, channels), jnp.bfloat16),
        in_specs=[pl.BlockSpec(memory_space=pltpu.VMEM)],
        out_specs=pl.BlockSpec(memory_space=pl.ANY),
        scratch_shapes=[dma((chunks,))],
        compiler_params=pltpu.CompilerParams(vmem_limit_bytes=8 << 20),
    )(mixed)


def solution(mesh):
    n = mesh.shape["seq"]
    rows = P(("rep", "seq"), None)
    return jax.shard_map(
        functools.partial(shards, n), mesh=mesh,
        in_specs=(rows, rows, rows, P(), P(), P()), out_specs=rows, check_vma=False)
```

```python
import functools

import jax
import jax.numpy as jnp
from jax import lax
from jax.experimental import pallas as pl
from jax.experimental.pallas import tpu as pltpu
from jax.sharding import PartitionSpec as P

GROUP_CH = 16
FILT = 128
FEAT = 3
LANES = 128
SUB = 16
CHUNK = 512
EARLY = 4
GRANT = 58 << 20
MESH = pl.DeviceIdType.MESH


def shifted(rim, x):
    ext = jnp.concatenate([rim, x], axis=0)
    return pltpu.roll(ext, 1, 0)[8:], pltpu.roll(ext, 2, 0)[8:]


def featurize(x, rim, taps):
    x = x.astype(jnp.float32)
    one, two = shifted(rim, x)
    return taps[0] * x + taps[1] * one + taps[2] * two


def kernel(
    n, q_hbm, k_hbm, v_hbm, feat_hbm, long_hbm, skip_hbm, mixed,
    q, k, v, feat, filt, skip, ends, kv_out, kv_in, q_out, q_in, gated, prev, toep,
    in_sem, end_sem, par_sem, send_sem, recv_sem,
):
    chunks, rows, width = gated.shape
    tiles = width // LANES
    groups = filt.shape[0]
    me = lax.axis_index("seq")
    right, left = lax.rem(me + 1, n), lax.rem(me + n - 1, n)
    has_left, has_right = me > 0, me < n - 1

    barrier = pltpu.get_barrier_semaphore()

    @pl.when(has_left)
    def _():
        pl.semaphore_signal(barrier, inc=1, device_id={"seq": left}, device_id_type=MESH)

    streams = ((k_hbm, k), (v_hbm, v), (q_hbm, q))

    def end_copy(i):
        return pltpu.make_async_copy(
            streams[i][0].at[pl.ds(rows - 8, 8)], ends.at[i], end_sem.at[i])

    def in_copy(i, c):
        cols = pl.ds(pl.multiple_of(c * width, width), width)
        return pltpu.make_async_copy(
            streams[i][0].at[:, cols], streams[i][1].at[c], in_sem.at[i, c])

    params = ((feat_hbm, feat), (long_hbm, filt), (skip_hbm, skip))

    def par_copy(i):
        return pltpu.make_async_copy(params[i][0], params[i][1], par_sem.at[i])

    in_copy(0, 0).start()
    in_copy(1, 0).start()
    par_copy(0).start()
    for i in range(3):
        end_copy(i).start()
    for c in range(1, EARLY):
        in_copy(0, c).start()
        in_copy(1, c).start()

    def remote(src, dst, slot):
        return pltpu.make_async_remote_copy(
            src_ref=src, dst_ref=dst, send_sem=send_sem.at[slot],
            recv_sem=recv_sem.at[slot], device_id={"seq": right}, device_id_type=MESH)

    def kv_copy():
        return remote(kv_out, kv_in, chunks + EARLY)

    def q_copy():
        return remote(q_out, q_in, chunks + EARLY + 1)

    def whole_copy(c):
        return remote(gated.at[c], prev.at[c], c)

    def body_copy(c):
        part = pl.ds(16, rows - 16)
        return remote(gated.at[c, part], prev.at[c, part], c)

    def head_copy(c):
        part = pl.ds(0, 16)
        return remote(gated.at[c, part], prev.at[c, part], chunks + c)

    row = lax.broadcasted_iota(jnp.int32, (8, LANES), 0)

    def last_rows(i, at):
        return ends[i, :, pl.ds(pl.multiple_of(at, LANES), LANES)].astype(jnp.float32)

    def pack_kv():
        half = kv_out.shape[1]

        @pl.loop(0, half // width)
        def _(c):
            for t in range(tiles):
                at = c * width + t * LANES
                packed = jnp.where(
                    row < 2, pltpu.roll(last_rows(0, at), 2, 0),
                    jnp.where(
                        row < 4, pltpu.roll(last_rows(1, at), 4, 0),
                        jnp.where(
                            row < 6, pltpu.roll(last_rows(0, at + half), 6, 0),
                            last_rows(1, at + half))))
                kv_out[:, pl.ds(pl.multiple_of(at, LANES), LANES)] = packed.astype(jnp.bfloat16)

    def pack_q():
        fourth = q_out.shape[1]

        @pl.loop(0, fourth // width)
        def _(c):
            for t in range(tiles):
                at = c * width + t * LANES
                packed = last_rows(2, at + 3 * fourth)
                for m in range(3):
                    packed = jnp.where(
                        row // 2 == m, pltpu.roll(last_rows(2, at + m * fourth), 2 + 2 * m, 0),
                        packed)
                q_out[:, pl.ds(pl.multiple_of(at, LANES), LANES)] = packed.astype(jnp.bfloat16)

    def taps_of(i, cols):
        return [feat[i, pl.ds(j, 1), cols] for j in range(FEAT)]

    def kv_rims(c, t):
        per_half = chunks // 2
        upper = c >= per_half
        at = lax.rem(c, per_half) * width + t * LANES
        x = kv_in[:, pl.ds(pl.multiple_of(at, LANES), LANES)].astype(jnp.float32)
        return (jnp.where(upper, pltpu.roll(x, 2, 0), pltpu.roll(x, 6, 0)),
                jnp.where(upper, x, pltpu.roll(x, 4, 0)))

    def q_rim(c, t):
        per_fourth = chunks // 4
        m = c // per_fourth
        at = lax.rem(c, per_fourth) * width + t * LANES
        x = q_in[:, pl.ds(pl.multiple_of(at, LANES), LANES)].astype(jnp.float32)
        rim = x
        for i in range(3):
            rim = jnp.where(m == i, pltpu.roll(x, 6 - 2 * i, 0), rim)
        return rim

    def columns(c, t):
        return pl.ds(pl.multiple_of(c * width + t * LANES, LANES), LANES)

    def gate(c, t, first, count, k_rim, v_rim):
        cols = columns(c, t)
        part, lanes = pl.ds(first, count), pl.ds(t * LANES, LANES)
        k_feat = featurize(k[c, part, lanes], k_rim, taps_of(1, cols))
        v_feat = featurize(v[c, part, lanes], v_rim, taps_of(2, cols))
        return (k_feat * v_feat).astype(jnp.bfloat16)

    zeros = jnp.zeros((8, LANES), jnp.float32)
    par_copy(0).wait()
    for c in range(EARLY):
        in_copy(0, c).wait()
        in_copy(1, c).wait()
        for t in range(tiles):
            lanes = pl.ds(t * LANES, LANES)
            gated[c, pl.ds(16, rows - 16), lanes] = gate(c, t, 0, rows, zeros, zeros)[16:]

        if c == 0:
            @pl.when(has_right)
            def _():
                pl.semaphore_wait(barrier, 1)
                body_copy(0).start()

            end_copy(0).wait()
            end_copy(1).wait()
            pack_kv()

            @pl.when(has_right)
            def _():
                kv_copy().start()
        else:
            @pl.when(has_right)
            def _():
                body_copy(c).start()

    @pl.loop(EARLY, chunks)
    def _(c):
        in_copy(0, c).start()
        in_copy(1, c).start()

    @pl.when(has_left)
    def _():
        kv_copy().wait_recv()

    @pl.when(jnp.logical_not(has_left))
    def _():
        kv_in[...] = jnp.zeros_like(kv_in)
        q_in[...] = jnp.zeros_like(q_in)

        @pl.loop(0, chunks)
        def _(c):
            prev[c] = jnp.zeros((rows, width), jnp.bfloat16)

    for c in range(EARLY):
        for t in range(tiles):
            gated[c, pl.ds(0, 16), pl.ds(t * LANES, LANES)] = gate(
                c, t, 0, 16, *kv_rims(c, t))

        @pl.when(has_right)
        def _():
            head_copy(c).start()

    end_copy(2).wait()
    pack_q()

    @pl.when(has_right)
    def _():
        q_copy().start()

    par_copy(1).start()
    par_copy(2).start()

    @pl.loop(0, chunks)
    def _(c):
        in_copy(2, c).start()

    @pl.loop(EARLY, chunks)
    def _(c):
        in_copy(0, c).wait()
        in_copy(1, c).wait()
        for t in range(tiles):
            gated[c, :, pl.ds(t * LANES, LANES)] = gate(c, t, 0, rows, *kv_rims(c, t))

        @pl.when(has_right)
        def _():
            whole_copy(c).start()

    par_copy(1).wait()
    par_copy(2).wait()
    taps = lax.broadcasted_iota(jnp.int32, (FILT, 2 * LANES), 0)
    place = lax.broadcasted_iota(jnp.int32, (FILT, 2 * LANES), 1)
    total = taps + place
    for b in range(SUB):
        onehot = jnp.where(total == FILT + b, 1.0, 0.0).astype(jnp.bfloat16)
        moved = jnp.dot(filt[...], onehot, preferred_element_type=jnp.float32)
        for r in range(2):
            toep[r, pl.ds(b, groups, stride=SUB), :] = moved[:, r * LANES:(r + 1) * LANES]

    lane_group = lax.broadcasted_iota(jnp.int32, (SUB, LANES), 1) // GROUP_CH
    per_tile = LANES // GROUP_CH
    blocks = rows // SUB
    depth = FILT + SUB

    def mix(c):
        for t in range(tiles):
            cols, lanes = columns(c, t), pl.ds(t * LANES, LANES)
            first = pl.multiple_of((c * tiles + t) * LANES, LANES)
            own = gated[c, :, lanes]
            window = jnp.concatenate([prev[c, :, lanes], own], axis=0)
            left_part = toep[0, pl.ds(first, LANES), :].astype(jnp.bfloat16)
            right_part = toep[1, pl.ds(first, LANES), :].astype(jnp.bfloat16)
            lhs = jnp.concatenate([left_part, right_part[:, :depth - LANES]], axis=1)
            rhs = jnp.concatenate(
                [window[a * SUB:a * SUB + depth] for a in range(blocks)], axis=1)
            every = jnp.dot(lhs, rhs, preferred_element_type=jnp.float32)
            conv = []
            for a in range(blocks):
                mine = every[:SUB, a * LANES:(a + 1) * LANES]
                for g in range(1, per_tile):
                    mine = jnp.where(
                        lane_group == g,
                        every[g * SUB:(g + 1) * SUB, a * LANES:(a + 1) * LANES], mine)
                conv.append(mine)
            conv = jnp.concatenate(conv, axis=0)
            q_feat = featurize(q[c, :, lanes], q_rim(c, t), taps_of(0, cols))
            direct = skip[:, cols] * own.astype(jnp.float32)
            mixed[c, :, lanes] = (q_feat * (conv + direct)).astype(jnp.bfloat16)

    @pl.when(has_left)
    def _():
        q_copy().wait_recv()

    for c in range(EARLY):
        @pl.when(has_left)
        def _():
            body_copy(c).wait_recv()
            head_copy(c).wait_recv()

        in_copy(2, c).wait()
        mix(c)

    @pl.loop(EARLY, chunks)
    def _(c):
        @pl.when(has_left)
        def _():
            whole_copy(c).wait_recv()

        in_copy(2, c).wait()
        mix(c)

    @pl.when(has_right)
    def _():
        kv_copy().wait_send()
        q_copy().wait_send()
        for c in range(EARLY):
            body_copy(c).wait_send()
            head_copy(c).wait_send()

        @pl.loop(EARLY, chunks)
        def _(c):
            whole_copy(c).wait_send()


def drain(mixed, out_hbm, sem):
    chunks, _, width = mixed.shape

    def copy(c):
        return pltpu.make_async_copy(
            mixed.at[c], out_hbm.at[:, c * width:(c + 1) * width], sem.at[c])

    for c in range(chunks):
        copy(c).start()
    for c in range(chunks):
        copy(c).wait()


def shards(n, q_stream, k_stream, v_stream, feat_filter, long_filter, skip_gain):
    rows, channels = q_stream.shape
    groups = long_filter.shape[0]
    chunks = channels // CHUNK
    cut = pltpu.VMEM((chunks, rows, CHUNK), jnp.bfloat16)
    dma = pltpu.SemaphoreType.DMA
    mixed = pl.pallas_call(
        functools.partial(kernel, n),
        out_shape=cut,
        in_specs=[pl.BlockSpec(memory_space=pltpu.HBM)] * 6,
        out_specs=pl.BlockSpec(memory_space=pltpu.VMEM),
        scratch_shapes=[
            cut, cut, cut,
            pltpu.VMEM(feat_filter.shape, jnp.float32),
            pltpu.VMEM(long_filter.shape, jnp.bfloat16),
            pltpu.VMEM((1, channels), jnp.float32),
            pltpu.VMEM((3, 8, channels), jnp.bfloat16),
            pltpu.VMEM((8, channels // 2), jnp.bfloat16),
            pltpu.VMEM((8, channels // 2), jnp.bfloat16),
            pltpu.VMEM((8, channels // 4), jnp.bfloat16),
            pltpu.VMEM((8, channels // 4), jnp.bfloat16),
            cut, cut,
            pltpu.VMEM((2, groups * SUB, LANES), jnp.float32),
            dma((3, chunks)), dma((3,)), dma((3,)),
            dma((chunks + EARLY + 2,)), dma((chunks + EARLY + 2,)),
        ],
        compiler_params=pltpu.CompilerParams(
            collective_id=0, has_side_effects=True, vmem_limit_bytes=GRANT),
    )(q_stream, k_stream, v_stream, feat_filter, long_filter, skip_gain.reshape(1, channels))
    return pl.pallas_call(
        drain,
        out_shape=jax.ShapeDtypeStruct((rows, channels), jnp.bfloat16),
        in_specs=[pl.BlockSpec(memory_space=pltpu.VMEM)],
        out_specs=pl.BlockSpec(memory_space=pl.ANY),
        scratch_shapes=[dma((chunks,))],
        compiler_params=pltpu.CompilerParams(vmem_limit_bytes=8 << 20),
    )(mixed)


def solution(mesh):
    n = mesh.shape["seq"]
    rows = P(("rep", "seq"), None)
    return jax.shard_map(
        functools.partial(shards, n), mesh=mesh,
        in_specs=(rows, rows, rows, P(), P(), P()), out_specs=rows, check_vma=False)
```

```python
import functools

import jax
import jax.numpy as jnp
from jax import lax
from jax.experimental import pallas as pl
from jax.experimental.pallas import tpu as pltpu
from jax.sharding import PartitionSpec as P

GROUP_CH = 16
FILT = 128
FEAT = 3
LANES = 128
SUB = 16
CHUNK = 512
EARLY = 4
GRANT = 58 << 20
MESH = pl.DeviceIdType.MESH


def shifted(rim, x):
    ext = jnp.concatenate([rim, x], axis=0)
    return pltpu.roll(ext, 1, 0)[8:], pltpu.roll(ext, 2, 0)[8:]


def featurize(x, rim, taps):
    x = x.astype(jnp.float32)
    one, two = shifted(rim, x)
    return taps[0] * x + taps[1] * one + taps[2] * two


def kernel(
    n, q_hbm, k_hbm, v_hbm, feat_hbm, long_hbm, skip_hbm, mixed,
    q, k, v, feat, filt, skip, ends, kv_out, kv_in, q_out, q_in, gated, prev, toep,
    in_sem, end_sem, par_sem, send_sem, recv_sem,
):
    chunks, rows, width = gated.shape
    tiles = width // LANES
    groups = filt.shape[0]
    me = lax.axis_index("seq")
    right, left = lax.rem(me + 1, n), lax.rem(me + n - 1, n)
    has_left, has_right = me > 0, me < n - 1

    barrier = pltpu.get_barrier_semaphore()

    @pl.when(has_left)
    def _():
        pl.semaphore_signal(barrier, inc=1, device_id={"seq": left}, device_id_type=MESH)

    streams = ((k_hbm, k), (v_hbm, v), (q_hbm, q))

    def end_copy(i):
        return pltpu.make_async_copy(
            streams[i][0].at[pl.ds(rows - 8, 8)], ends.at[i], end_sem.at[i])

    def in_copy(i, c):
        cols = pl.ds(pl.multiple_of(c * width, width), width)
        return pltpu.make_async_copy(
            streams[i][0].at[:, cols], streams[i][1].at[c], in_sem.at[i, c])

    params = ((feat_hbm, feat), (long_hbm, filt), (skip_hbm, skip))

    def par_copy(i):
        return pltpu.make_async_copy(params[i][0], params[i][1], par_sem.at[i])

    in_copy(0, 0).start()
    in_copy(1, 0).start()
    par_copy(0).start()
    for i in range(3):
        end_copy(i).start()
    for c in range(1, EARLY):
        in_copy(0, c).start()
        in_copy(1, c).start()

    def remote(src, dst, slot):
        return pltpu.make_async_remote_copy(
            src_ref=src, dst_ref=dst, send_sem=send_sem.at[slot],
            recv_sem=recv_sem.at[slot], device_id={"seq": right}, device_id_type=MESH)

    def kv_copy():
        return remote(kv_out, kv_in, chunks + EARLY)

    def q_copy():
        return remote(q_out, q_in, chunks + EARLY + 1)

    def whole_copy(c):
        return remote(gated.at[c], prev.at[c], c)

    def body_copy(c):
        part = pl.ds(16, rows - 16)
        return remote(gated.at[c, part], prev.at[c, part], c)

    last = chunks - 1
    spare = chunks + EARLY + 2

    def first_copy(h):
        part, lanes = pl.ds(16, rows - 16), pl.ds(h * (width // 2), width // 2)
        return remote(gated.at[0, part, lanes], prev.at[0, part, lanes], spare + h)

    def last_copy(t):
        lanes = pl.ds(t * LANES, LANES)
        return remote(gated.at[last, :, lanes], prev.at[last, :, lanes], spare + 2 + t)

    def head_copy(c):
        part = pl.ds(0, 16)
        return remote(gated.at[c, part], prev.at[c, part], chunks + c)

    row = lax.broadcasted_iota(jnp.int32, (8, LANES), 0)

    def last_rows(i, at):
        return ends[i, :, pl.ds(pl.multiple_of(at, LANES), LANES)].astype(jnp.float32)

    def pack_kv():
        half = kv_out.shape[1]

        @pl.loop(0, half // width)
        def _(c):
            for t in range(tiles):
                at = c * width + t * LANES
                packed = jnp.where(
                    row < 2, pltpu.roll(last_rows(0, at), 2, 0),
                    jnp.where(
                        row < 4, pltpu.roll(last_rows(1, at), 4, 0),
                        jnp.where(
                            row < 6, pltpu.roll(last_rows(0, at + half), 6, 0),
                            last_rows(1, at + half))))
                kv_out[:, pl.ds(pl.multiple_of(at, LANES), LANES)] = packed.astype(jnp.bfloat16)

    def pack_q():
        fourth = q_out.shape[1]

        @pl.loop(0, fourth // width)
        def _(c):
            for t in range(tiles):
                at = c * width + t * LANES
                packed = last_rows(2, at + 3 * fourth)
                for m in range(3):
                    packed = jnp.where(
                        row // 2 == m, pltpu.roll(last_rows(2, at + m * fourth), 2 + 2 * m, 0),
                        packed)
                q_out[:, pl.ds(pl.multiple_of(at, LANES), LANES)] = packed.astype(jnp.bfloat16)

    def taps_of(i, cols):
        return [feat[i, pl.ds(j, 1), cols] for j in range(FEAT)]

    def kv_rims(c, t):
        per_half = chunks // 2
        upper = c >= per_half
        at = lax.rem(c, per_half) * width + t * LANES
        x = kv_in[:, pl.ds(pl.multiple_of(at, LANES), LANES)].astype(jnp.float32)
        return (jnp.where(upper, pltpu.roll(x, 2, 0), pltpu.roll(x, 6, 0)),
                jnp.where(upper, x, pltpu.roll(x, 4, 0)))

    def q_rim(c, t):
        per_fourth = chunks // 4
        m = c // per_fourth
        at = lax.rem(c, per_fourth) * width + t * LANES
        x = q_in[:, pl.ds(pl.multiple_of(at, LANES), LANES)].astype(jnp.float32)
        rim = x
        for i in range(3):
            rim = jnp.where(m == i, pltpu.roll(x, 6 - 2 * i, 0), rim)
        return rim

    def columns(c, t):
        return pl.ds(pl.multiple_of(c * width + t * LANES, LANES), LANES)

    def gate(c, t, first, count, k_rim, v_rim):
        cols = columns(c, t)
        part, lanes = pl.ds(first, count), pl.ds(t * LANES, LANES)
        k_feat = featurize(k[c, part, lanes], k_rim, taps_of(1, cols))
        v_feat = featurize(v[c, part, lanes], v_rim, taps_of(2, cols))
        return (k_feat * v_feat).astype(jnp.bfloat16)

    zeros = jnp.zeros((8, LANES), jnp.float32)
    par_copy(0).wait()
    for c in range(EARLY):
        in_copy(0, c).wait()
        in_copy(1, c).wait()
        for t in range(tiles):
            lanes = pl.ds(t * LANES, LANES)
            gated[c, pl.ds(16, rows - 16), lanes] = gate(c, t, 0, rows, zeros, zeros)[16:]
            if c == 0 and t == tiles // 2 - 1:
                @pl.when(has_right)
                def _():
                    pl.semaphore_wait(barrier, 1)
                    first_copy(0).start()

        if c == 0:
            @pl.when(has_right)
            def _():
                first_copy(1).start()

            end_copy(0).wait()
            end_copy(1).wait()
            pack_kv()

            @pl.when(has_right)
            def _():
                kv_copy().start()
        else:
            @pl.when(has_right)
            def _():
                body_copy(c).start()

    @pl.loop(EARLY, chunks)
    def _(c):
        in_copy(0, c).start()
        in_copy(1, c).start()

    @pl.when(has_left)
    def _():
        kv_copy().wait_recv()

    @pl.when(jnp.logical_not(has_left))
    def _():
        kv_in[...] = jnp.zeros_like(kv_in)
        q_in[...] = jnp.zeros_like(q_in)

        @pl.loop(0, chunks)
        def _(c):
            prev[c] = jnp.zeros((rows, width), jnp.bfloat16)

    for c in range(EARLY):
        for t in range(tiles):
            gated[c, pl.ds(0, 16), pl.ds(t * LANES, LANES)] = gate(
                c, t, 0, 16, *kv_rims(c, t))

        @pl.when(has_right)
        def _():
            head_copy(c).start()

    end_copy(2).wait()
    pack_q()

    @pl.when(has_right)
    def _():
        q_copy().start()

    par_copy(1).start()
    par_copy(2).start()

    @pl.loop(0, chunks)
    def _(c):
        in_copy(2, c).start()

    @pl.loop(EARLY, chunks)
    def _(c):
        in_copy(0, c).wait()
        in_copy(1, c).wait()
        for t in range(tiles):
            gated[c, :, pl.ds(t * LANES, LANES)] = gate(c, t, 0, rows, *kv_rims(c, t))

        @pl.when(jnp.logical_and(has_right, c < last))
        def _():
            whole_copy(c).start()

    @pl.when(has_right)
    def _():
        for t in range(tiles):
            last_copy(t).start()

    par_copy(1).wait()
    par_copy(2).wait()
    taps = lax.broadcasted_iota(jnp.int32, (FILT, 2 * LANES), 0)
    place = lax.broadcasted_iota(jnp.int32, (FILT, 2 * LANES), 1)
    total = taps + place
    for b in range(SUB):
        onehot = jnp.where(total == FILT + b, 1.0, 0.0).astype(jnp.bfloat16)
        moved = jnp.dot(filt[...], onehot, preferred_element_type=jnp.float32)
        for r in range(2):
            toep[r, pl.ds(b, groups, stride=SUB), :] = moved[:, r * LANES:(r + 1) * LANES]

    lane_group = lax.broadcasted_iota(jnp.int32, (SUB, LANES), 1) // GROUP_CH
    per_tile = LANES // GROUP_CH
    blocks = rows // SUB
    depth = FILT + SUB

    def mix(c, only=None):
        for t in range(tiles) if only is None else (only,):
            cols, lanes = columns(c, t), pl.ds(t * LANES, LANES)
            first = pl.multiple_of((c * tiles + t) * LANES, LANES)
            own = gated[c, :, lanes]
            window = jnp.concatenate([prev[c, :, lanes], own], axis=0)
            left_part = toep[0, pl.ds(first, LANES), :].astype(jnp.bfloat16)
            right_part = toep[1, pl.ds(first, LANES), :].astype(jnp.bfloat16)
            lhs = jnp.concatenate([left_part, right_part[:, :depth - LANES]], axis=1)
            rhs = jnp.concatenate(
                [window[a * SUB:a * SUB + depth] for a in range(blocks)], axis=1)
            every = jnp.dot(lhs, rhs, preferred_element_type=jnp.float32)
            conv = []
            for a in range(blocks):
                mine = every[:SUB, a * LANES:(a + 1) * LANES]
                for g in range(1, per_tile):
                    mine = jnp.where(
                        lane_group == g,
                        every[g * SUB:(g + 1) * SUB, a * LANES:(a + 1) * LANES], mine)
                conv.append(mine)
            conv = jnp.concatenate(conv, axis=0)
            q_feat = featurize(q[c, :, lanes], q_rim(c, t), taps_of(0, cols))
            direct = skip[:, cols] * own.astype(jnp.float32)
            mixed[c, :, lanes] = (q_feat * (conv + direct)).astype(jnp.bfloat16)

    @pl.when(has_left)
    def _():
        q_copy().wait_recv()

    for c in range(EARLY):
        @pl.when(has_left)
        def _():
            if c == 0:
                first_copy(0).wait_recv()
                first_copy(1).wait_recv()
            else:
                body_copy(c).wait_recv()
            head_copy(c).wait_recv()

        in_copy(2, c).wait()
        mix(c)

    @pl.loop(EARLY, last)
    def _(c):
        @pl.when(has_left)
        def _():
            whole_copy(c).wait_recv()

        in_copy(2, c).wait()
        mix(c)

    in_copy(2, last).wait()
    for t in range(tiles):
        @pl.when(has_left)
        def _():
            last_copy(t).wait_recv()

        mix(last, t)

    @pl.when(has_right)
    def _():
        kv_copy().wait_send()
        q_copy().wait_send()
        first_copy(0).wait_send()
        first_copy(1).wait_send()
        head_copy(0).wait_send()
        for c in range(1, EARLY):
            body_copy(c).wait_send()
            head_copy(c).wait_send()

        @pl.loop(EARLY, last)
        def _(c):
            whole_copy(c).wait_send()

        for t in range(tiles):
            last_copy(t).wait_send()


def drain(mixed, out_hbm, sem):
    chunks, _, width = mixed.shape

    def copy(c):
        return pltpu.make_async_copy(
            mixed.at[c], out_hbm.at[:, c * width:(c + 1) * width], sem.at[c])

    for c in range(chunks):
        copy(c).start()
    for c in range(chunks):
        copy(c).wait()


def shards(n, q_stream, k_stream, v_stream, feat_filter, long_filter, skip_gain):
    rows, channels = q_stream.shape
    groups = long_filter.shape[0]
    chunks = channels // CHUNK
    cut = pltpu.VMEM((chunks, rows, CHUNK), jnp.bfloat16)
    dma = pltpu.SemaphoreType.DMA
    remotes = chunks + EARLY + 4 + CHUNK // LANES
    mixed = pl.pallas_call(
        functools.partial(kernel, n),
        out_shape=cut,
        in_specs=[pl.BlockSpec(memory_space=pltpu.HBM)] * 6,
        out_specs=pl.BlockSpec(memory_space=pltpu.VMEM),
        scratch_shapes=[
            cut, cut, cut,
            pltpu.VMEM(feat_filter.shape, jnp.float32),
            pltpu.VMEM(long_filter.shape, jnp.bfloat16),
            pltpu.VMEM((1, channels), jnp.float32),
            pltpu.VMEM((3, 8, channels), jnp.bfloat16),
            pltpu.VMEM((8, channels // 2), jnp.bfloat16),
            pltpu.VMEM((8, channels // 2), jnp.bfloat16),
            pltpu.VMEM((8, channels // 4), jnp.bfloat16),
            pltpu.VMEM((8, channels // 4), jnp.bfloat16),
            cut, cut,
            pltpu.VMEM((2, groups * SUB, LANES), jnp.float32),
            dma((3, chunks)), dma((3,)), dma((3,)),
            dma((remotes,)), dma((remotes,)),
        ],
        compiler_params=pltpu.CompilerParams(
            collective_id=0, has_side_effects=True, vmem_limit_bytes=GRANT),
    )(q_stream, k_stream, v_stream, feat_filter, long_filter, skip_gain.reshape(1, channels))
    return pl.pallas_call(
        drain,
        out_shape=jax.ShapeDtypeStruct((rows, channels), jnp.bfloat16),
        in_specs=[pl.BlockSpec(memory_space=pltpu.VMEM)],
        out_specs=pl.BlockSpec(memory_space=pl.ANY),
        scratch_shapes=[dma((chunks,))],
        compiler_params=pltpu.CompilerParams(vmem_limit_bytes=8 << 20),
    )(mixed)


def solution(mesh):
    n = mesh.shape["seq"]
    rows = P(("rep", "seq"), None)
    return jax.shard_map(
        functools.partial(shards, n), mesh=mesh,
        in_specs=(rows, rows, rows, P(), P(), P()), out_specs=rows, check_vma=False)
```

```python
import functools

import jax
import jax.numpy as jnp
from jax import lax
from jax.experimental import pallas as pl
from jax.experimental.pallas import tpu as pltpu
from jax.sharding import PartitionSpec as P

GROUP_CH = 16
FILT = 128
FEAT = 3
LANES = 128
SUB = 16
CHUNK = 512
EARLY = 4
GRANT = 58 << 20
MESH = pl.DeviceIdType.MESH


def shifted(rim, x):
    ext = jnp.concatenate([rim, x], axis=0)
    return pltpu.roll(ext, 1, 0)[8:], pltpu.roll(ext, 2, 0)[8:]


def featurize(x, rim, taps):
    x = x.astype(jnp.float32)
    one, two = shifted(rim, x)
    return taps[0] * x + taps[1] * one + taps[2] * two


def kernel(
    n, q_hbm, k_hbm, v_hbm, feat_hbm, long_hbm, skip_hbm, mixed,
    q, k, v, feat, filt, skip, ends, kv_out, kv_in, q_out, q_in, gated, prev, toep,
    in_sem, end_sem, par_sem, send_sem, recv_sem,
):
    chunks, rows, width = gated.shape
    tiles = width // LANES
    groups = filt.shape[0]
    me = lax.axis_index("seq")
    right, left = lax.rem(me + 1, n), lax.rem(me + n - 1, n)
    has_left, has_right = me > 0, me < n - 1

    barrier = pltpu.get_barrier_semaphore()

    @pl.when(has_left)
    def _():
        pl.semaphore_signal(barrier, inc=1, device_id={"seq": left}, device_id_type=MESH)

    streams = ((k_hbm, k), (v_hbm, v), (q_hbm, q))

    def end_copy(i):
        return pltpu.make_async_copy(
            streams[i][0].at[pl.ds(rows - 8, 8)], ends.at[i], end_sem.at[i])

    def in_copy(i, c):
        cols = pl.ds(pl.multiple_of(c * width, width), width)
        return pltpu.make_async_copy(
            streams[i][0].at[:, cols], streams[i][1].at[c], in_sem.at[i, c])

    params = ((feat_hbm, feat), (long_hbm, filt), (skip_hbm, skip))

    def par_copy(i):
        return pltpu.make_async_copy(params[i][0], params[i][1], par_sem.at[i])

    def feat_copy(first, count):
        cols = pl.ds(first, count)
        return pltpu.make_async_copy(
            feat_hbm.at[:, :, cols], feat.at[:, :, cols],
            par_sem.at[0] if first == 0 else par_sem.at[3])

    in_copy(0, 0).start()
    in_copy(1, 0).start()
    feat_copy(0, width).start()
    for i in range(2):
        end_copy(i).start()
    feat_copy(width, chunks * width - width).start()
    end_copy(2).start()
    for c in range(1, EARLY):
        in_copy(0, c).start()
        in_copy(1, c).start()

    def remote(src, dst, slot):
        return pltpu.make_async_remote_copy(
            src_ref=src, dst_ref=dst, send_sem=send_sem.at[slot],
            recv_sem=recv_sem.at[slot], device_id={"seq": right}, device_id_type=MESH)

    def kv_copy():
        return remote(kv_out, kv_in, chunks + EARLY)

    def q_copy():
        return remote(q_out, q_in, chunks + EARLY + 1)

    def whole_copy(c):
        return remote(gated.at[c], prev.at[c], c)

    def body_copy(c):
        part = pl.ds(16, rows - 16)
        return remote(gated.at[c, part], prev.at[c, part], c)

    def head_copy(c):
        part = pl.ds(0, 16)
        return remote(gated.at[c, part], prev.at[c, part], chunks + c)

    row = lax.broadcasted_iota(jnp.int32, (8, LANES), 0)

    def last_rows(i, at):
        return ends[i, :, pl.ds(pl.multiple_of(at, LANES), LANES)].astype(jnp.float32)

    def pack_kv():
        half = kv_out.shape[1]

        @pl.loop(0, half // width)
        def _(c):
            for t in range(tiles):
                at = c * width + t * LANES
                packed = jnp.where(
                    row < 2, pltpu.roll(last_rows(0, at), 2, 0),
                    jnp.where(
                        row < 4, pltpu.roll(last_rows(1, at), 4, 0),
                        jnp.where(
                            row < 6, pltpu.roll(last_rows(0, at + half), 6, 0),
                            last_rows(1, at + half))))
                kv_out[:, pl.ds(pl.multiple_of(at, LANES), LANES)] = packed.astype(jnp.bfloat16)

    def pack_q():
        fourth = q_out.shape[1]

        @pl.loop(0, fourth // width)
        def _(c):
            for t in range(tiles):
                at = c * width + t * LANES
                packed = last_rows(2, at + 3 * fourth)
                for m in range(3):
                    packed = jnp.where(
                        row // 2 == m, pltpu.roll(last_rows(2, at + m * fourth), 2 + 2 * m, 0),
                        packed)
                q_out[:, pl.ds(pl.multiple_of(at, LANES), LANES)] = packed.astype(jnp.bfloat16)

    def taps_of(i, cols):
        return [feat[i, pl.ds(j, 1), cols] for j in range(FEAT)]

    def kv_rims(c, t):
        per_half = chunks // 2
        upper = c >= per_half
        at = lax.rem(c, per_half) * width + t * LANES
        x = kv_in[:, pl.ds(pl.multiple_of(at, LANES), LANES)].astype(jnp.float32)
        return (jnp.where(upper, pltpu.roll(x, 2, 0), pltpu.roll(x, 6, 0)),
                jnp.where(upper, x, pltpu.roll(x, 4, 0)))

    def q_rim(c, t):
        per_fourth = chunks // 4
        m = c // per_fourth
        at = lax.rem(c, per_fourth) * width + t * LANES
        x = q_in[:, pl.ds(pl.multiple_of(at, LANES), LANES)].astype(jnp.float32)
        rim = x
        for i in range(3):
            rim = jnp.where(m == i, pltpu.roll(x, 6 - 2 * i, 0), rim)
        return rim

    def columns(c, t):
        return pl.ds(pl.multiple_of(c * width + t * LANES, LANES), LANES)

    def gate(c, t, first, count, k_rim, v_rim):
        cols = columns(c, t)
        part, lanes = pl.ds(first, count), pl.ds(t * LANES, LANES)
        k_feat = featurize(k[c, part, lanes], k_rim, taps_of(1, cols))
        v_feat = featurize(v[c, part, lanes], v_rim, taps_of(2, cols))
        return (k_feat * v_feat).astype(jnp.bfloat16)

    zeros = jnp.zeros((8, LANES), jnp.float32)
    feat_copy(0, width).wait()
    for c in range(EARLY):
        if c == 1:
            feat_copy(width, chunks * width - width).wait()
        in_copy(0, c).wait()
        in_copy(1, c).wait()
        for t in range(tiles):
            lanes = pl.ds(t * LANES, LANES)
            gated[c, pl.ds(16, rows - 16), lanes] = gate(c, t, 0, rows, zeros, zeros)[16:]

        if c == 0:
            @pl.when(has_right)
            def _():
                pl.semaphore_wait(barrier, 1)
                body_copy(0).start()

            end_copy(0).wait()
            end_copy(1).wait()
            pack_kv()

            @pl.when(has_right)
            def _():
                kv_copy().start()
        else:
            @pl.when(has_right)
            def _():
                body_copy(c).start()

    @pl.loop(EARLY, chunks)
    def _(c):
        in_copy(0, c).start()
        in_copy(1, c).start()

    @pl.when(has_left)
    def _():
        kv_copy().wait_recv()

    @pl.when(jnp.logical_not(has_left))
    def _():
        kv_in[...] = jnp.zeros_like(kv_in)
        q_in[...] = jnp.zeros_like(q_in)

        @pl.loop(0, chunks)
        def _(c):
            prev[c] = jnp.zeros((rows, width), jnp.bfloat16)

    for c in range(EARLY):
        for t in range(tiles):
            gated[c, pl.ds(0, 16), pl.ds(t * LANES, LANES)] = gate(
                c, t, 0, 16, *kv_rims(c, t))

        @pl.when(has_right)
        def _():
            head_copy(c).start()

    end_copy(2).wait()
    pack_q()

    @pl.when(has_right)
    def _():
        q_copy().start()

    par_copy(1).start()
    par_copy(2).start()

    @pl.loop(0, chunks)
    def _(c):
        in_copy(2, c).start()

    @pl.loop(EARLY, chunks)
    def _(c):
        in_copy(0, c).wait()
        in_copy(1, c).wait()
        for t in range(tiles):
            gated[c, :, pl.ds(t * LANES, LANES)] = gate(c, t, 0, rows, *kv_rims(c, t))

        @pl.when(has_right)
        def _():
            whole_copy(c).start()

    par_copy(1).wait()
    par_copy(2).wait()
    taps = lax.broadcasted_iota(jnp.int32, (FILT, 2 * LANES), 0)
    place = lax.broadcasted_iota(jnp.int32, (FILT, 2 * LANES), 1)
    total = taps + place
    for b in range(SUB):
        onehot = jnp.where(total == FILT + b, 1.0, 0.0).astype(jnp.bfloat16)
        moved = jnp.dot(filt[...], onehot, preferred_element_type=jnp.float32)
        for r in range(2):
            toep[r, pl.ds(b, groups, stride=SUB), :] = moved[:, r * LANES:(r + 1) * LANES]

    lane_group = lax.broadcasted_iota(jnp.int32, (SUB, LANES), 1) // GROUP_CH
    per_tile = LANES // GROUP_CH
    blocks = rows // SUB
    depth = FILT + SUB

    def mix(c):
        for t in range(tiles):
            cols, lanes = columns(c, t), pl.ds(t * LANES, LANES)
            first = pl.multiple_of((c * tiles + t) * LANES, LANES)
            own = gated[c, :, lanes]
            window = jnp.concatenate([prev[c, :, lanes], own], axis=0)
            left_part = toep[0, pl.ds(first, LANES), :].astype(jnp.bfloat16)
            right_part = toep[1, pl.ds(first, LANES), :].astype(jnp.bfloat16)
            lhs = jnp.concatenate([left_part, right_part[:, :depth - LANES]], axis=1)
            rhs = jnp.concatenate(
                [window[a * SUB:a * SUB + depth] for a in range(blocks)], axis=1)
            every = jnp.dot(lhs, rhs, preferred_element_type=jnp.float32)
            conv = []
            for a in range(blocks):
                mine = every[:SUB, a * LANES:(a + 1) * LANES]
                for g in range(1, per_tile):
                    mine = jnp.where(
                        lane_group == g,
                        every[g * SUB:(g + 1) * SUB, a * LANES:(a + 1) * LANES], mine)
                conv.append(mine)
            conv = jnp.concatenate(conv, axis=0)
            q_feat = featurize(q[c, :, lanes], q_rim(c, t), taps_of(0, cols))
            direct = skip[:, cols] * own.astype(jnp.float32)
            mixed[:, cols] = (q_feat * (conv + direct)).astype(jnp.bfloat16)

    @pl.when(has_left)
    def _():
        q_copy().wait_recv()

    for c in range(EARLY):
        @pl.when(has_left)
        def _():
            body_copy(c).wait_recv()
            head_copy(c).wait_recv()

        in_copy(2, c).wait()
        mix(c)

    @pl.loop(EARLY, chunks)
    def _(c):
        @pl.when(has_left)
        def _():
            whole_copy(c).wait_recv()

        in_copy(2, c).wait()
        mix(c)

    @pl.when(has_right)
    def _():
        kv_copy().wait_send()
        q_copy().wait_send()
        for c in range(EARLY):
            body_copy(c).wait_send()
            head_copy(c).wait_send()

        @pl.loop(EARLY, chunks)
        def _(c):
            whole_copy(c).wait_send()


def drain(mixed, out_hbm, sem):
    blocks = sem.shape[0]
    height = mixed.shape[0] // blocks

    def copy(b):
        part = pl.ds(b * height, height)
        return pltpu.make_async_copy(mixed.at[part], out_hbm.at[part], sem.at[b])

    for b in range(blocks):
        copy(b).start()
    for b in range(blocks):
        copy(b).wait()


def shards(n, q_stream, k_stream, v_stream, feat_filter, long_filter, skip_gain):
    rows, channels = q_stream.shape
    groups = long_filter.shape[0]
    chunks = channels // CHUNK
    cut = pltpu.VMEM((chunks, rows, CHUNK), jnp.bfloat16)
    dma = pltpu.SemaphoreType.DMA
    mixed = pl.pallas_call(
        functools.partial(kernel, n),
        out_shape=pltpu.VMEM((rows, channels), jnp.bfloat16),
        in_specs=[pl.BlockSpec(memory_space=pltpu.HBM)] * 6,
        out_specs=pl.BlockSpec(memory_space=pltpu.VMEM),
        scratch_shapes=[
            cut, cut, cut,
            pltpu.VMEM(feat_filter.shape, jnp.float32),
            pltpu.VMEM(long_filter.shape, jnp.bfloat16),
            pltpu.VMEM((1, channels), jnp.float32),
            pltpu.VMEM((3, 8, channels), jnp.bfloat16),
            pltpu.VMEM((8, channels // 2), jnp.bfloat16),
            pltpu.VMEM((8, channels // 2), jnp.bfloat16),
            pltpu.VMEM((8, channels // 4), jnp.bfloat16),
            pltpu.VMEM((8, channels // 4), jnp.bfloat16),
            cut, cut,
            pltpu.VMEM((2, groups * SUB, LANES), jnp.float32),
            dma((3, chunks)), dma((3,)), dma((4,)),
            dma((chunks + EARLY + 2,)), dma((chunks + EARLY + 2,)),
        ],
        compiler_params=pltpu.CompilerParams(
            collective_id=0, has_side_effects=True, vmem_limit_bytes=GRANT),
    )(q_stream, k_stream, v_stream, feat_filter, long_filter, skip_gain.reshape(1, channels))
    return pl.pallas_call(
        drain,
        out_shape=jax.ShapeDtypeStruct((rows, channels), jnp.bfloat16),
        in_specs=[pl.BlockSpec(memory_space=pltpu.VMEM)],
        out_specs=pl.BlockSpec(memory_space=pl.ANY),
        scratch_shapes=[dma((rows // 16,))],
        compiler_params=pltpu.CompilerParams(vmem_limit_bytes=8 << 20),
    )(mixed)


def solution(mesh):
    n = mesh.shape["seq"]
    rows = P(("rep", "seq"), None)
    return jax.shard_map(
        functools.partial(shards, n), mesh=mesh,
        in_specs=(rows, rows, rows, P(), P(), P()), out_specs=rows, check_vma=False)
```
